256 devices in a mesh: rows: 256 (over y, z, x, core).
Axes of the slice: x: 4, y: 4, z: 8, core: 2. Of those that a mesh axis runs over, the one named last changes fastest.
Arguments:
- features: bfloat16 [1048576, 440], P('rows'), may hold values from -6 to 6
- residual: float32 [1048576], P('rows')
- block_index: int32 [1024], replicated, may hold values from 0 to 1048575, as said below
Outputs:
- updated: float32 [1048576], P('rows')
- coefficient: float32 [1024], replicated
- rms_value: float32 [], replicated
The draws below stay inside these ranges and needn't reach their ends.
Inputs may be any that keep to these rules, and one draw needn't show every extreme that they name: `block_index`: 1024 distinct frame indices; no device's range of 4096 frames holds more than 8 of them, and some device holds exactly 8.
All inputs are finite; a program needn't handle non-finite values.
Results may differ from the reference program's by a relative error of at most 0.0003.
Values may be sent and summed in bfloat16 or wider, within the bound.
A program may use at most 128 MiB of HBM per device.

```python
import jax
import jax.numpy as jnp
from jax import lax

FEAT = 440
BLOCK = 1024
ROWS_DEV = 4096
TOTAL = 1048576
MOST = 8


def draw_block_index(key, part):
    device_list = TOTAL // ROWS_DEV
    grid = device_list * MOST
    key_noise = jax.random.fold_in(key, 11)
    reward_key = jax.random.fold_in(key, 12)
    key_forced = jax.random.fold_in(key, 13)
    key_base = jax.random.fold_in(key, 14)
    ordering_key = jax.random.fold_in(key, 15)
    slot_jitter = jax.random.randint(key_noise, (grid,), 0, 2 ** 16)
    device_reward = jax.random.randint(reward_key, (device_list,), 0, 2 ** 16)
    forced = jax.random.randint(key_forced, (), 0, device_list)
    slot_ids = jnp.arange(grid, dtype=jnp.int32)
    device_for_row = slot_ids // MOST
    ranking_score = slot_jitter + device_reward[device_for_row] + 1
    ranking_score = jnp.where(device_for_row == forced, 0, ranking_score)
    ranked = jnp.argsort(ranking_score * grid + slot_ids, stable=True)
    picks = ranked[:BLOCK]
    owner = picks // MOST
    within = picks % MOST
    base = jax.random.randint(key_base, (device_list,), 0, ROWS_DEV)
    offset = (within * (ROWS_DEV // MOST) + base[owner]) % ROWS_DEV
    chosen = owner * ROWS_DEV + offset
    order = jax.random.permutation(ordering_key, BLOCK)
    return chosen[order].astype(jnp.int32)


def draw_residual(key, part):
    where_at = jnp.arange(TOTAL, dtype=jnp.float32) / max(TOTAL - 1, 1)
    base_vals = jax.random.truncated_normal(key, -5.0, 5.0, (TOTAL,), jnp.float32)
    return (base_vals * (1.0 + where_at)).astype(jnp.float32)


def level_of(rng, extent, pieces, least, top_value):
    gain, own = 1.0, jax.random.fold_in(rng, 6)
    for position, shards_of in pieces:
        steps = jnp.exp(jax.random.uniform(jax.random.fold_in(own, position), (shards_of,), jnp.float32, least / len(pieces), top_value / len(pieces)))
        gain = gain * jnp.repeat(steps, extent[position] // shards_of).reshape([-1 if axis == position else 1 for axis in range(len(extent))])
    return gain


def bell_draw(key, shape, width, most, pieces=(), kind=jnp.bfloat16):
    drawn = width * jax.random.normal(key, shape, jnp.float32)
    if pieces:
        drawn = drawn * level_of(key, shape, pieces, -0.22, 0.18)
    return jnp.clip(drawn, -most, most).astype(kind)


def setup_inputs(seed: int = 0) -> dict:
    splits = jax.random.split(jax.random.key(seed), 4)
    features = bell_draw(splits[0], (TOTAL, FEAT), 1.0, 6.0, ((0, 256),))
    residual = draw_residual(jax.random.fold_in(splits[3], 71), 0)
    block_index = draw_block_index(jax.random.fold_in(splits[3], 71), 0)
    return dict(features=features, residual=residual, block_index=block_index)


def kernel_of(left, right, left_norm, right_norm, scale):
    inner = jnp.dot(left.astype(jnp.float32), right.T.astype(jnp.float32), preferred_element_type=jnp.float32)
    return jnp.exp(-scale * (left_norm[:, None] + right_norm[None, :] - 2.0 * inner))

def chol_apply(factor, target):
    column = target[:, None]
    forward = lax.linalg.triangular_solve(factor, column, left_side=True, lower=True)
    backward = lax.linalg.triangular_solve(factor, forward, left_side=True, lower=True, transpose_a=True)
    return backward[:, 0]

def reference(features, residual, block_index):
    scale = 2.0 / FEAT
    block_feat = features[block_index]
    block_res = residual[block_index]
    block_norm = lax.optimization_barrier(jnp.sum(jnp.square(block_feat.astype(jnp.float32)), axis=1))
    system = kernel_of(block_feat, block_feat, block_norm, block_norm, scale)
    system = system + 0.1 * jnp.eye(BLOCK, dtype=jnp.float32)
    factor = jnp.linalg.cholesky(system)
    coefficient = chol_apply(factor, block_res)
    block_rows = min(1024, ROWS_DEV)
    grouped = features.reshape(TOTAL // block_rows, block_rows, FEAT)

    def one_block(rows_in):
        row_norm = lax.optimization_barrier(jnp.sum(jnp.square(rows_in.astype(jnp.float32)), axis=1))
        panel = kernel_of(rows_in, block_feat, row_norm, block_norm, scale)
        return jnp.dot(panel, coefficient, precision=lax.Precision.HIGHEST)
    change = lax.map(one_block, grouped).reshape(TOTAL)
    updated = residual - change
    rms_value = jnp.sqrt(jnp.sum(updated * updated) / TOTAL + 1e-06)
    return (updated, coefficient, rms_value)
```

```python
import functools

import jax
import jax.numpy as jnp
from jax import lax
from jax.experimental import pallas as pl
from jax.experimental.pallas import tpu as pltpu
from jax.sharding import PartitionSpec as P

F32 = jnp.float32
BF16 = jnp.bfloat16
LANES = 128
MOST = 8
WIDE = 512
LOG2E = 1.4426950408889634


def pieces(value):
    high = value.astype(BF16).astype(F32)
    rest = value - high
    mid = rest.astype(BF16).astype(F32)
    low = (rest - mid).astype(BF16).astype(F32)
    return high, mid, low


def lane_of(shape):
    return lax.broadcasted_iota(jnp.int32, shape, 1)


def eye_mask():
    return lax.broadcasted_iota(jnp.int32, (LANES, LANES), 0) == lane_of((LANES, LANES))


def to_column(row, eye):
    return jnp.sum(jnp.where(eye, row, 0.0), axis=1, keepdims=True)


def to_row(column, eye):
    return jnp.sum(jnp.where(eye, column, 0.0), axis=0, keepdims=True)


def total(value):
    return jnp.sum(jnp.sum(value, axis=1, keepdims=True), axis=0, keepdims=True)


def solve_kernel(local_rows, width, scale, shift, idx_ref, g_ref, b_ref, coef_ref, place, system):
    size = b_ref.shape[0]
    groups = size // LANES
    slots = g_ref.shape[0]
    base = WIDE - LANES
    col = width - base
    eye = eye_mask()
    owner = (idx_ref[...] // local_rows).astype(F32)
    lower = lane_of((LANES, LANES)) < lax.broadcasted_iota(jnp.int32, (LANES, LANES), 0)
    for t in range(groups):
        mine = to_column(owner[t : t + 1, :], eye)
        count = jnp.where((mine == owner[t : t + 1, :]) & lower, 1.0, 0.0)
        for u in range(t):
            count = count + jnp.where(mine == owner[u : u + 1, :], 1.0, 0.0)
        slot = mine * MOST + jnp.sum(count, axis=1, keepdims=True)
        slot = slot.astype(jnp.int32)
        place[t * LANES : (t + 1) * LANES, :] = jnp.where(
            lane_of((LANES, slots)) == slot, 1.0, 0.0
        ).astype(BF16)
    block = jnp.dot(place[...], g_ref[...], preferred_element_type=F32)
    tail = block[:, base:]
    lane = lane_of(tail.shape)
    target_cols = jnp.sum(
        jnp.where((lane >= col + 6) & (lane < col + 9), tail, 0.0), axis=1, keepdims=True
    )
    tail = jnp.where(lane < col + 6, tail, 0.0)
    moved = pltpu.roll(tail, 3, 1)
    swap = jnp.where(lane < col, tail, jnp.where(lane < col + 3, 1.0, jnp.where(lane < col + 6, moved, 0.0)))
    b_ref[:, :base] = block[:, :base].astype(BF16)
    b_ref[:, base:] = tail.astype(BF16)
    place[:, :base] = block[:, :base].astype(BF16)
    place[:, base:WIDE] = swap.astype(BF16)
    inner = lax.dot_general(
        b_ref[...], place[:, :WIDE], (((1,), (1,)), ((), ())), preferred_element_type=F32
    )
    system[...] = jnp.exp2(inner * (2.0 * scale * LOG2E))
    for t in range(groups):
        here = slice(t * LANES, (t + 1) * LANES)
        system[here, here] = system[here, here] + jnp.where(eye, shift, 0.0)

    target = jnp.concatenate(
        [to_row(target_cols[t * LANES : (t + 1) * LANES], eye) for t in range(groups)], axis=0
    )
    top = jnp.max(jnp.max(jnp.abs(target), axis=1, keepdims=True), axis=0, keepdims=True)
    top = jnp.where(top > 0.0, top, 1.0)
    target = target / top

    def apply(p):
        rows = []
        for t in range(groups):
            acc = system[t * LANES : (t + 1) * LANES, :LANES] * p[:1, :]
            for u in range(1, groups):
                acc = acc + system[t * LANES : (t + 1) * LANES, u * LANES : (u + 1) * LANES] * p[u : u + 1, :]
            rows.append(to_row(jnp.sum(acc, axis=1, keepdims=True), eye))
        return jnp.concatenate(rows, axis=0)

    first = total(target * target)
    bound = first * 1e-12

    def going(carry):
        step, _, _, _, norm = carry
        return (step < 4 * size) & (jnp.sum(norm - bound) > 0.0)

    def advance(carry):
        step, x, r, p, norm = carry
        q = apply(p)
        alpha = norm / total(p * q)
        x = x + alpha * p
        r = r - alpha * q
        fresh = total(r * r)
        p = r + (fresh / norm) * p
        return step + 1, x, r, p, fresh

    out = lax.while_loop(
        going, advance, (jnp.int32(0), jnp.zeros_like(target), target, target, first)
    )
    coef_ref[...] = out[1] * top


def widen(rows):
    width = rows.shape[1]
    base = WIDE - LANES
    col = width - base
    value = rows.astype(F32)
    square = value * value
    parts = square[:, :LANES]
    for t in range(1, base // LANES):
        parts = parts + square[:, t * LANES : (t + 1) * LANES]
    tail = jnp.concatenate(
        [value[:, base:], jnp.zeros((rows.shape[0], LANES - col), F32)], axis=1
    )
    parts = parts + tail * tail
    half = -0.5 * jnp.sum(parts, axis=1, keepdims=True)
    high, mid, low = pieces(half)
    lane = lane_of(tail.shape)
    extra = jnp.where(
        lane < col + 3,
        1.0,
        jnp.where(lane == col + 3, high, jnp.where(lane == col + 4, mid, jnp.where(lane == col + 5, low, 0.0))),
    )
    return jnp.where(lane < col, tail, extra).astype(BF16)


def panel_kernel(tile, scale, coef_ref, b_ref, x_ref, res_ref, out_ref, sum_ref, wide, columns):
    rows, width = x_ref.shape
    size = b_ref.shape[0]
    base = WIDE - LANES
    eye = eye_mask()
    for t in range(size // LANES):
        columns[t * LANES : (t + 1) * LANES, :] = jnp.broadcast_to(
            to_column(coef_ref[t : t + 1, :], eye), (LANES, LANES)
        )

    def step(i, _):
        here = pl.ds(pl.multiple_of(i * tile, tile), tile)
        wide[:, :base] = x_ref[here, :base]
        wide[:, base:] = widen(x_ref[here, :])
        inner = lax.dot_general(
            b_ref[...], wide[...], (((1,), (1,)), ((), ())), preferred_element_type=F32
        )
        value = jnp.exp2(inner * (2.0 * scale * LOG2E))
        for k in range(tile // LANES):
            change = jnp.sum(value[:, k * LANES : (k + 1) * LANES] * columns[...], axis=0, keepdims=True)
            at = pl.ds(i * (tile // LANES) + k, 1)
            out_ref[at, :] = res_ref[at, :] - change
        return 0

    lax.fori_loop(0, rows // tile, step, 0)
    updated = out_ref[...]
    square = updated * updated
    parts = square[:8, :]
    for t in range(1, square.shape[0] // 8):
        parts = parts + square[t * 8 : (t + 1) * 8, :]
    sum_ref[...] = jnp.broadcast_to(total(parts), sum_ref.shape)


VM = pl.BlockSpec(memory_space=pltpu.VMEM)


def solve(idx, gathered, local_rows, width, scale):
    size = idx.shape[0]
    return pl.pallas_call(
        functools.partial(solve_kernel, local_rows, width, scale, 0.1),
        out_shape=(
            jax.ShapeDtypeStruct((size, WIDE), BF16),
            jax.ShapeDtypeStruct((size // LANES, LANES), F32),
        ),
        in_specs=[VM, VM],
        out_specs=(VM, VM),
        scratch_shapes=[
            pltpu.VMEM((size, gathered.shape[0]), BF16),
            pltpu.VMEM((size, size), F32),
        ],
        compiler_params=pltpu.CompilerParams(vmem_limit_bytes=40 << 20),
        name="solve",
    )(idx.reshape(size // LANES, LANES), gathered)


def panel(coef, block, features, residual, scale):
    rows, width = features.shape
    size = block.shape[0]
    tile = 256
    return pl.pallas_call(
        functools.partial(panel_kernel, tile, scale),
        out_shape=(
            jax.ShapeDtypeStruct((rows // LANES, LANES), F32),
            jax.ShapeDtypeStruct((8, LANES), F32),
        ),
        in_specs=[VM, VM, VM, VM],
        out_specs=(VM, VM),
        scratch_shapes=[
            pltpu.VMEM((tile, WIDE), BF16),
            pltpu.VMEM((size, LANES), F32),
        ],
        compiler_params=pltpu.CompilerParams(vmem_limit_bytes=40 << 20),
        name="panel",
    )(coef, block, features, residual.reshape(rows // LANES, LANES))


def rounded(value):
    return lax.reduce_precision(value, 8, 7)


def slots_of(features, residual, block_index):
    local_rows, width = features.shape
    own = lax.axis_index("rows")
    mine = block_index // local_rows == own
    rank = jnp.cumsum(mine.astype(jnp.int32)) - 1
    hit = mine[None, :] & (rank[None, :] == jnp.arange(MOST)[:, None])
    offset = jnp.sum(jnp.where(hit, (block_index - own * local_rows)[None, :], 0), axis=1)
    found = jnp.any(hit, axis=1)[:, None]
    rows = jnp.where(found, features[offset].astype(F32), 0.0)
    res = jnp.where(found, residual[offset][:, None], 0.0)
    half = -0.5 * jnp.sum(rows * rows, axis=1, keepdims=True)

    def split(value):
        high = rounded(value)
        mid = rounded(value - high)
        return [high, mid, rounded(value - high - mid)]

    ones = jnp.where(found, jnp.ones((MOST, 3), F32), 0.0)
    return jnp.concatenate(
        [rows] + split(half) + [ones] + split(res) + [jnp.zeros((MOST, WIDE - width - 9), F32)], axis=1
    ).astype(BF16)


def on_device(features, residual, block_index):
    local_rows, width = features.shape
    scale = 2.0 / width
    mine = slots_of(features, residual, block_index)
    gathered = lax.all_gather(mine, "rows", axis=0, tiled=True)
    block, coef = solve(block_index, gathered, local_rows, width, scale)
    updated, square = panel(coef, block, features, residual, scale)
    square_sum = lax.psum(square[0, 0], "rows")
    frame_count = local_rows * lax.axis_size("rows")
    rms_value = jnp.sqrt(square_sum / frame_count + 1e-06)
    return (updated.reshape(local_rows), coef.reshape(-1), rms_value)


def solution(mesh):
    in_specs = (P("rows", None), P("rows"), P())
    out_specs = (P("rows"), P(), P())
    return jax.shard_map(
        on_device, mesh=mesh, in_specs=in_specs, out_specs=out_specs, check_vma=False
    )
```

```python
import functools

import jax
import jax.numpy as jnp
from jax import lax
from jax.experimental import pallas as pl
from jax.experimental.pallas import tpu as pltpu
from jax.sharding import PartitionSpec as P

F32 = jnp.float32
BF16 = jnp.bfloat16
LANES = 128
MOST = 8
WIDE = 512
LOG2E = 1.4426950408889634
GRID = (4, 8, 4)
DEEP = 448
MESH = pl.DeviceIdType.MESH


def pieces(value):
    high = value.astype(BF16).astype(F32)
    rest = value - high
    mid = rest.astype(BF16).astype(F32)
    low = (rest - mid).astype(BF16).astype(F32)
    return high, mid, low


def lane_of(shape):
    return lax.broadcasted_iota(jnp.int32, shape, 1)


def eye_mask():
    return lax.broadcasted_iota(jnp.int32, (LANES, LANES), 0) == lane_of((LANES, LANES))


def to_column(row, eye):
    return jnp.sum(jnp.where(eye, row, 0.0), axis=1, keepdims=True)


def to_row(column, eye):
    return jnp.sum(jnp.where(eye, column, 0.0), axis=0, keepdims=True)


def total(value):
    return jnp.sum(jnp.sum(value, axis=1, keepdims=True), axis=0, keepdims=True)


def position():
    me = lax.axis_index("rows")
    core = lax.rem(me, 2)
    x = lax.rem(me // 2, GRID[2])
    z = lax.rem(me // (2 * GRID[2]), GRID[1])
    y = me // (2 * GRID[2] * GRID[1])
    return me, y, z, x, core


def device(y, z, x, core):
    return ((y * GRID[1] + z) * GRID[2] + x) * 2 + core


def signal(barrier, target):
    pl.semaphore_signal(barrier, inc=1, device_id=(target,), device_id_type=MESH)


def send_to(src, dst, send_sem, recv_sem, target):
    return pltpu.make_async_remote_copy(
        src_ref=src, dst_ref=dst, send_sem=send_sem, recv_sem=recv_sem,
        device_id=(target,), device_id_type=MESH,
    )


def own_offsets(idx, me, local_rows):
    size = idx.shape[0] * LANES
    mine = jnp.where(idx // local_rows == me, 1.0, 0.0)
    sub = lax.broadcasted_iota(jnp.int32, (LANES, LANES), 0)
    before = jnp.where(sub < lane_of((LANES, LANES)), 1.0, 0.0)
    rank = jnp.dot(mine, before, preferred_element_type=F32)
    count = jnp.sum(mine, axis=1, keepdims=True)
    row = lax.broadcasted_iota(jnp.int32, idx.shape, 0)
    for t in range(idx.shape[0] - 1):
        rank = rank + jnp.where(row > t, count[t : t + 1, :], 0.0)
    offset = (idx - me * local_rows + 1).astype(F32)
    return [
        total(jnp.where((mine > 0.0) & (rank == s), offset, 0.0)) - 1.0 for s in range(MOST)
    ]


def stacked(values):
    sub = lax.broadcasted_iota(jnp.int32, (MOST, 1), 0)
    out = jnp.broadcast_to(values[0], (MOST, 1))
    for s in range(1, MOST):
        out = jnp.where(sub == s, values[s], out)
    return out


def gather_kernel(
    local_rows, idx_ref, x_hbm, res_ref, xa_ref, block_ref,
    xs, place, pair, own, other, load_sem, pair_sem, far_send, far_recv, two_send, two_recv,
    three_send, three_recv, relay_send, relay_recv, swap_send, swap_recv,
):
    width = xs.shape[0]
    size = block_ref.shape[0]
    base = WIDE - LANES
    half = WIDE // 2
    chunks = load_sem.shape[0]
    step = local_rows // chunks
    me, y, z, x, core = position()
    two = core * y + (1 - core) * x
    three = core * x + (1 - core) * y
    ring = GRID[0]
    deep = GRID[1]
    partner = device(y, z, x, 1 - core)

    def on_z(v):
        return device(y, v, x, core)

    def on_two(v):
        return device(core * v + (1 - core) * y, z, core * x + (1 - core) * v, core)

    def on_three(v):
        return device(core * y + (1 - core) * v, z, core * v + (1 - core) * x, core)

    def turn(v, by, n):
        return lax.rem(v + by + n, n)

    plus, minus = on_three(turn(three, 1, ring)), on_three(turn(three, -1, ring))

    barrier = pltpu.get_barrier_semaphore()
    signal(barrier, partner)
    for d in range(1, deep):
        signal(barrier, on_z(turn(z, d, deep)))
    for d in range(1, ring):
        signal(barrier, on_two(turn(two, d, ring)))
    signal(barrier, plus)
    signal(barrier, minus)

    loads = []
    for c in range(chunks):
        here = slice(c * step, (c + 1) * step)
        loads.append(pltpu.make_async_copy(x_hbm.at[:, here], xs.at[:, here], load_sem.at[c]))
        loads[-1].start()

    idx = idx_ref[...]
    offsets = own_offsets(idx, me, local_rows)
    column = stacked(offsets)
    frame = (
        lax.broadcasted_iota(jnp.int32, res_ref.shape, 0) * LANES + lane_of(res_ref.shape)
    ).astype(F32)
    target = stacked([total(jnp.where(frame == v, res_ref[...], 0.0)) for v in offsets])
    rows = None
    for c in range(chunks):
        loads[c].wait()
        hot = jnp.where(
            lane_of((MOST, step)).astype(F32) + float(c * step) == column, 1.0, 0.0
        ).astype(BF16)
        part = lax.dot_general(
            hot, xs[:, c * step : (c + 1) * step], (((1,), (1,)), ((), ())),
            preferred_element_type=F32,
        )
        rows = part if rows is None else rows + part
    col = width - base
    tail = jnp.concatenate([rows[:, base:], jnp.zeros((MOST, LANES - col), F32)], axis=1)
    square = tail * tail
    for t in range(base // LANES):
        square = square + rows[:, t * LANES : (t + 1) * LANES] * rows[:, t * LANES : (t + 1) * LANES]
    norm = pieces(-0.5 * jnp.sum(square, axis=1, keepdims=True))
    wanted = pieces(target)
    lane = lane_of(tail.shape)
    for k in range(3):
        tail = jnp.where(lane == col + k, norm[k], tail)
        tail = jnp.where(lane == col + 3 + k, 1.0, tail)
        tail = jnp.where(lane == col + 6 + k, wanted[k], tail)
    pair[core, :, :base] = rows[:, :base]
    pair[core, :, base:] = tail

    pl.semaphore_wait(barrier, 1 + (deep - 1) + (ring - 1) + 2)

    first = send_to(pair.at[core], pair.at[core], pair_sem.at[0], pair_sem.at[1], partner)
    first.start()
    first.wait()
    mine = pl.ds(pl.multiple_of(core * half, half), half)
    both = jnp.concatenate([pair[0, :, mine], pair[1, :, mine]], axis=0)
    own[three, two, z] = both.astype(BF16)

    waits = []
    far = []
    for d in range(1, deep):
        there = own.at[three, two, z]
        far.append(send_to(there, there, far_send.at[d - 1], far_recv.at[d - 1], on_z(turn(z, d, deep))))
        far[-1].start()
    waits += far

    eye = eye_mask()
    owner = idx // local_rows
    row_owner = owner.astype(F32)
    home = lax.rem(owner, 2) * MOST + lax.rem(owner // (2 * GRID[2]), deep) * (2 * MOST)
    on_x = lax.rem(owner // 2, GRID[2])
    on_y = owner // (2 * GRID[2] * deep)
    spans = (2 * MOST * deep * ring, 2 * MOST * deep)
    slot_own = (home + (core * on_x + (1 - core) * on_y) * spans[0] + (core * on_y + (1 - core) * on_x) * spans[1]).astype(F32)
    slot_other = (home + (core * on_y + (1 - core) * on_x) * spans[0] + (core * on_x + (1 - core) * on_y) * spans[1]).astype(F32)
    lower = lane_of((LANES, LANES)) < lax.broadcasted_iota(jnp.int32, (LANES, LANES), 0)
    slots = place.shape[2]
    for t in range(size // LANES):
        here = slice(t * LANES, (t + 1) * LANES)
        holder = to_column(row_owner[t : t + 1, :], eye)
        count = jnp.where((holder == row_owner[t : t + 1, :]) & lower, 1.0, 0.0)
        for u in range(t):
            count = count + jnp.where(holder == row_owner[u : u + 1, :], 1.0, 0.0)
        rank = jnp.sum(count, axis=1, keepdims=True)
        for k, slot in enumerate((slot_own, slot_other)):
            at = (to_column(slot[t : t + 1, :], eye) + rank).astype(jnp.int32)
            place[k, here, :] = jnp.where(lane_of((LANES, slots)) == at, 1.0, 0.0).astype(BF16)

    def widen(c):
        here = slice(c * step, (c + 1) * step)
        value = xs[:, here].astype(F32)
        square = value * value
        parts = square[:8, :]
        for t in range(1, width // 8):
            parts = parts + square[t * 8 : (t + 1) * 8, :]
        norm = pieces(-0.5 * jnp.sum(parts, axis=0, keepdims=True))
        sub = lax.broadcasted_iota(jnp.int32, (8, step), 0)
        extra = jnp.where(sub < 3, 1.0, 0.0)
        for k in range(3):
            extra = jnp.where(sub == 3 + k, norm[k], extra)
        xa_ref[: width - 8, here] = xs[: width - 8, here]
        xa_ref[width - 8 :, here] = jnp.concatenate([value[width - 8 :, :], extra], axis=0).astype(BF16)

    other_cols = pl.ds(pl.multiple_of((1 - core) * half, half), half)

    def add_block(which, index, start):
        buf, cols = (own, mine) if which == 0 else (other, other_cols)
        k = pl.ds(pl.multiple_of(index * spans[0], spans[0]), spans[0])
        part = jnp.dot(
            place[which, :, k], buf[index].reshape(spans[0], half), preferred_element_type=F32
        )
        if start:
            block_ref[:, cols] = part
        else:
            block_ref[:, cols] = block_ref[:, cols] + part

    swaps = {}

    def swap(a, b):
        i, j = turn(three, a, ring), turn(two, b, ring)
        n = a * ring + b
        swaps[a, b] = send_to(own.at[i, j], other.at[i, j], swap_send.at[n], swap_recv.at[n], partner)
        swaps[a, b].start()

    straight = {}

    def onward(b):
        there = own.at[three, turn(two, b, ring)]
        for k, goal in enumerate((plus, minus)):
            copy = send_to(there, there, three_send.at[k, b], three_recv.at[k, b], goal)
            copy.start()
            straight[k, b] = copy

    relays = {}

    def relay(k, b):
        there = own.at[turn(three, -1 if k == 0 else 1, ring), turn(two, b, ring)]
        n = {0: 0, 1: 1, 3: 2, 2: 3}[b]
        copy = send_to(there, there, relay_send.at[n], relay_recv.at[n], plus if k == 0 else minus)
        copy.start()
        relays[b] = copy

    for copy in far:
        copy.wait_recv()
    second = {}
    for d in (1, 3, 2):
        there = own.at[three, two]
        second[d] = send_to(there, there, two_send.at[d - 1], two_recv.at[d - 1], on_two(turn(two, -d, ring)))
        second[d].start()
    onward(0)
    swap(0, 0)
    for c in range(chunks // 2):
        widen(c)
    for d in (1, 3):
        second[d].wait_recv()
        onward(d)
        swap(0, d)
    straight[0, 0].wait_recv()
    relay(0, 0)
    swap(3, 0)
    straight[1, 0].wait_recv()
    swap(1, 0)
    second[2].wait_recv()
    onward(2)
    swap(0, 2)
    add_block(0, three, True)
    straight[0, 1].wait_recv()
    relay(0, 1)
    swap(3, 1)
    straight[1, 3].wait_recv()
    relay(1, 3)
    swap(1, 3)
    straight[1, 1].wait_recv()
    swap(1, 1)
    straight[0, 3].wait_recv()
    swap(3, 3)
    for c in range(chunks // 2, chunks):
        widen(c)
    straight[1, 2].wait_recv()
    relay(1, 2)
    swap(1, 2)
    straight[0, 2].wait_recv()
    swap(3, 2)
    add_block(0, turn(three, 1, ring), False)
    add_block(0, turn(three, -1, ring), False)
    for b in range(ring):
        swaps[0, b].wait_recv()
    add_block(1, two, True)
    for b in (0, 1, 3, 2):
        relays[b].wait_recv()
        swap(2, b)
    add_block(0, turn(three, 2, ring), False)
    for a in (1, 3, 2):
        for b in range(ring):
            swaps[a, b].wait_recv()
        add_block(1, turn(two, a, ring), False)
    for copy in waits + list(second.values()) + list(straight.values()) + list(relays.values()) + list(swaps.values()):
        copy.wait_send()


def solve_kernel(width, scale, shift, block_ref, b_ref, coef_ref, swapped, system):
    size = b_ref.shape[0]
    groups = size // LANES
    base = WIDE - LANES
    col = width - base
    eye = eye_mask()
    tail = block_ref[:, base:]
    lane = lane_of(tail.shape)
    target_cols = jnp.sum(
        jnp.where((lane >= col + 6) & (lane < col + 9), tail, 0.0), axis=1, keepdims=True
    )
    tail = jnp.where(lane < col + 6, tail, 0.0)
    moved = pltpu.roll(tail, 3, 1)
    swap = jnp.where(lane < col, tail, jnp.where(lane < col + 3, 1.0, jnp.where(lane < col + 6, moved, 0.0)))
    plain = block_ref[:, :base].astype(BF16)
    b_ref[:, :base] = plain
    b_ref[:, base:] = tail.astype(BF16)
    swapped[:, :base] = plain
    swapped[:, base:] = swap.astype(BF16)
    inner = lax.dot_general(
        b_ref[...], swapped[...], (((1,), (1,)), ((), ())), preferred_element_type=F32
    )
    system[...] = jnp.exp2(inner * (2.0 * scale * LOG2E))
    for t in range(groups):
        here = slice(t * LANES, (t + 1) * LANES)
        system[here, here] = system[here, here] + jnp.where(eye, shift, 0.0)

    target = jnp.concatenate(
        [to_row(target_cols[t * LANES : (t + 1) * LANES], eye) for t in range(groups)], axis=0
    )
    top = jnp.max(jnp.max(jnp.abs(target), axis=1, keepdims=True), axis=0, keepdims=True)
    top = jnp.where(top > 0.0, top, 1.0)
    target = target / top

    def apply(p):
        rows = []
        for t in range(groups):
            acc = system[t * LANES : (t + 1) * LANES, :LANES] * p[:1, :]
            for u in range(1, groups):
                acc = acc + system[t * LANES : (t + 1) * LANES, u * LANES : (u + 1) * LANES] * p[u : u + 1, :]
            rows.append(to_row(jnp.sum(acc, axis=1, keepdims=True), eye))
        return jnp.concatenate(rows, axis=0)

    first = total(target * target)
    bound = first * 1e-12

    def going(carry):
        step, _, _, _, norm = carry
        return (step < 4 * size) & (jnp.sum(norm - bound) > 0.0)

    def advance(carry):
        step, x, r, p, norm = carry
        q = apply(p)
        alpha = norm / total(p * q)
        x = x + alpha * p
        r = r - alpha * q
        fresh = total(r * r)
        p = r + (fresh / norm) * p
        return step + 1, x, r, p, fresh

    out = lax.while_loop(
        going, advance, (jnp.int32(0), jnp.zeros_like(target), target, target, first)
    )
    coef_ref[...] = out[1] * top


def panel_kernel(
    tile, scale, frames, coef_ref, b_ref, x_ref, res_ref, out_ref, rms_ref,
    columns, line_a, line_b, send_a, recv_a, send_b, recv_b,
):
    rows = x_ref.shape[1]
    size = b_ref.shape[0]
    me, y, z, x, core = position()
    spot_a = z * 2 + core
    spot_b = y * GRID[2] + x
    count_a = line_a.shape[0]
    count_b = line_b.shape[0]

    def peer_a(d):
        v = lax.rem(spot_a + d, count_a)
        return device(y, v // 2, x, lax.rem(v, 2))

    def peer_b(d):
        v = lax.rem(spot_b + d, count_b)
        return device(v // GRID[2], z, lax.rem(v, GRID[2]), core)

    barrier = pltpu.get_barrier_semaphore()

    def greet_a(d, _):
        signal(barrier, peer_a(d))
        return 0

    def greet_b(d, _):
        signal(barrier, peer_b(d))
        return 0

    lax.fori_loop(1, count_a, greet_a, 0)
    lax.fori_loop(1, count_b, greet_b, 0)

    eye = eye_mask()
    for t in range(size // LANES):
        columns[t * LANES : (t + 1) * LANES, :] = jnp.broadcast_to(
            to_column(coef_ref[t : t + 1, :], eye), (LANES, LANES)
        )

    def step(i, _):
        here = pl.ds(pl.multiple_of(i * tile, tile), tile)
        inner = jnp.dot(b_ref[:, :DEEP], x_ref[:, here], preferred_element_type=F32)
        value = jnp.exp2(inner * (2.0 * scale * LOG2E))
        for k in range(tile // LANES):
            change = jnp.sum(value[:, k * LANES : (k + 1) * LANES] * columns[...], axis=0, keepdims=True)
            at = pl.ds(i * (tile // LANES) + k, 1)
            out_ref[at, :] = res_ref[at, :] - change
        return 0

    lax.fori_loop(0, rows // tile, step, 0)
    updated = out_ref[...]
    square = updated * updated
    parts = square[:8, :]
    for t in range(1, square.shape[0] // 8):
        parts = parts + square[t * 8 : (t + 1) * 8, :]
    line_a[spot_a] = jnp.broadcast_to(total(parts), (1, LANES))

    pl.semaphore_wait(barrier, count_a + count_b - 2)

    def exchange(line, spot, send, recv, peer):
        def copy(d):
            return send_to(line.at[spot], line.at[spot], send.at[d - 1], recv.at[d - 1], peer(d))

        def begin(d, _):
            copy(d).start()
            return 0

        def end(d, _):
            copy(d).wait()
            return 0

        lax.fori_loop(1, line.shape[0], begin, 0)
        lax.fori_loop(1, line.shape[0], end, 0)
        out = line[0]
        for k in range(1, line.shape[0]):
            out = out + line[k]
        return out

    line_b[spot_b] = exchange(line_a, spot_a, send_a, recv_a, peer_a)
    whole = exchange(line_b, spot_b, send_b, recv_b, peer_b)
    rms_ref[...] = jnp.sqrt(whole / frames + 1e-06)


VM = pl.BlockSpec(memory_space=pltpu.VMEM)
DMA = pltpu.SemaphoreType.DMA


def gather(idx, features, residual):
    width, local_rows = features.shape
    size = idx.shape[0]
    slots = 2 * GRID[0] * GRID[1] * GRID[2] * MOST
    part = (GRID[0], GRID[2], GRID[1], 2 * MOST, WIDE // 2)
    return pl.pallas_call(
        functools.partial(gather_kernel, local_rows),
        out_shape=(
            jax.ShapeDtypeStruct((DEEP, local_rows), BF16),
            jax.ShapeDtypeStruct((size, WIDE), F32),
        ),
        in_specs=[VM, pl.BlockSpec(memory_space=pl.ANY), VM],
        out_specs=(VM, VM),
        scratch_shapes=[
            pltpu.VMEM((width, local_rows), BF16),
            pltpu.VMEM((2, size, slots), BF16),
            pltpu.VMEM((2, MOST, WIDE), F32),
            pltpu.VMEM(part, BF16),
            pltpu.VMEM(part, BF16),
            DMA((4,)),
            DMA((2,)),
            DMA((GRID[1] - 1,)),
            DMA((GRID[1] - 1,)),
            DMA((3,)),
            DMA((3,)),
            DMA((2, 4)),
            DMA((2, 4)),
            DMA((4,)),
            DMA((4,)),
            DMA((16,)),
            DMA((16,)),
        ],
        compiler_params=pltpu.CompilerParams(
            vmem_limit_bytes=36 << 20, collective_id=0, has_side_effects=True
        ),
        name="gather",
    )(idx.reshape(size // LANES, LANES), features, residual.reshape(local_rows // LANES, LANES))


def solve(block, width, scale):
    size = block.shape[0]
    return pl.pallas_call(
        functools.partial(solve_kernel, width, scale, 0.1),
        out_shape=(
            jax.ShapeDtypeStruct((size, WIDE), BF16),
            jax.ShapeDtypeStruct((size // LANES, LANES), F32),
        ),
        in_specs=[VM],
        out_specs=(VM, VM),
        scratch_shapes=[
            pltpu.VMEM((size, WIDE), BF16),
            pltpu.VMEM((size, size), F32),
        ],
        compiler_params=pltpu.CompilerParams(vmem_limit_bytes=36 << 20),
        name="solve",
    )(block)


def panel(coef, block, wide, residual, scale):
    rows = wide.shape[1]
    size = block.shape[0]
    tile = 256
    return pl.pallas_call(
        functools.partial(panel_kernel, tile, scale, float(rows * lax.axis_size("rows"))),
        out_shape=(
            jax.ShapeDtypeStruct((rows // LANES, LANES), F32),
            jax.ShapeDtypeStruct((1, LANES), F32),
        ),
        in_specs=[VM, VM, VM, VM],
        out_specs=(VM, VM),
        scratch_shapes=[
            pltpu.VMEM((size, LANES), F32),
            pltpu.VMEM((2 * GRID[1], 1, LANES), F32),
            pltpu.VMEM((GRID[0] * GRID[2], 1, LANES), F32),
            DMA((15,)),
            DMA((15,)),
            DMA((15,)),
            DMA((15,)),
        ],
        compiler_params=pltpu.CompilerParams(
            vmem_limit_bytes=36 << 20, collective_id=1, has_side_effects=True
        ),
        name="panel",
    )(coef, block, wide, residual.reshape(rows // LANES, LANES))


def on_device(features, residual, block_index):
    local_rows, width = features.shape
    scale = 2.0 / width
    wide, block = gather(block_index, features.T, residual)
    block, coef = solve(block, width, scale)
    updated, rms = panel(coef, block, wide, residual, scale)
    return (updated.reshape(local_rows), coef.reshape(-1), rms[0, 0])


def solution(mesh):
    in_specs = (P("rows", None), P("rows"), P())
    out_specs = (P("rows"), P(), P())
    return jax.shard_map(
        on_device, mesh=mesh, in_specs=in_specs, out_specs=out_specs, check_vma=False
    )
```

```python
import functools

import jax
import jax.numpy as jnp
from jax import lax
from jax.experimental import pallas as pl
from jax.experimental.pallas import tpu as pltpu
from jax.sharding import PartitionSpec as P

F32 = jnp.float32
BF16 = jnp.bfloat16
LANES = 128
MOST = 8
WIDE = 512
LOG2E = 1.4426950408889634
GRID = (4, 8, 4)
DEEP = 448
MESH = pl.DeviceIdType.MESH


def pieces(value):
    high = value.astype(BF16).astype(F32)
    rest = value - high
    mid = rest.astype(BF16).astype(F32)
    low = (rest - mid).astype(BF16).astype(F32)
    return high, mid, low


def lane_of(shape):
    return lax.broadcasted_iota(jnp.int32, shape, 1)


def eye_mask():
    return lax.broadcasted_iota(jnp.int32, (LANES, LANES), 0) == lane_of((LANES, LANES))


def to_column(row, eye):
    return jnp.sum(jnp.where(eye, row, 0.0), axis=1, keepdims=True)


def to_row(column, eye):
    return jnp.sum(jnp.where(eye, column, 0.0), axis=0, keepdims=True)


def total(value):
    return jnp.sum(jnp.sum(value, axis=1, keepdims=True), axis=0, keepdims=True)


def position():
    me = lax.axis_index("rows")
    core = lax.rem(me, 2)
    x = lax.rem(me // 2, GRID[2])
    z = lax.rem(me // (2 * GRID[2]), GRID[1])
    y = me // (2 * GRID[2] * GRID[1])
    return me, y, z, x, core


def device(y, z, x, core):
    return ((y * GRID[1] + z) * GRID[2] + x) * 2 + core


def signal(barrier, target):
    pl.semaphore_signal(barrier, inc=1, device_id=(target,), device_id_type=MESH)


def send_to(src, dst, send_sem, recv_sem, target):
    return pltpu.make_async_remote_copy(
        src_ref=src, dst_ref=dst, send_sem=send_sem, recv_sem=recv_sem,
        device_id=(target,), device_id_type=MESH,
    )


def own_offsets(idx, me, local_rows):
    size = idx.shape[0] * LANES
    mine = jnp.where(idx // local_rows == me, 1.0, 0.0)
    sub = lax.broadcasted_iota(jnp.int32, (LANES, LANES), 0)
    before = jnp.where(sub < lane_of((LANES, LANES)), 1.0, 0.0)
    rank = jnp.dot(mine, before, preferred_element_type=F32)
    count = jnp.sum(mine, axis=1, keepdims=True)
    row = lax.broadcasted_iota(jnp.int32, idx.shape, 0)
    for t in range(idx.shape[0] - 1):
        rank = rank + jnp.where(row > t, count[t : t + 1, :], 0.0)
    offset = (idx - me * local_rows + 1).astype(F32)
    return [
        total(jnp.where((mine > 0.0) & (rank == s), offset, 0.0)) - 1.0 for s in range(MOST)
    ]


def stacked(values):
    sub = lax.broadcasted_iota(jnp.int32, (MOST, 1), 0)
    out = jnp.broadcast_to(values[0], (MOST, 1))
    for s in range(1, MOST):
        out = jnp.where(sub == s, values[s], out)
    return out


def gather_kernel(
    local_rows, idx_hbm, x_hbm, res_hbm, xa_ref, block_ref,
    idx_ref, res_ref, small_sem, xs, place, pair, own, other, load_sem, pair_sem, far_send, far_recv, two_send, two_recv,
    three_send, three_recv, relay_send, relay_recv, swap_send, swap_recv,
):
    width = xs.shape[0]
    size = block_ref.shape[0]
    base = WIDE - LANES
    half = WIDE // 2
    chunks = load_sem.shape[0]
    step = local_rows // chunks
    me, y, z, x, core = position()
    two = core * y + (1 - core) * x
    three = core * x + (1 - core) * y
    ring = GRID[0]
    deep = GRID[1]
    partner = device(y, z, x, 1 - core)

    def on_z(v):
        return device(y, v, x, core)

    def on_two(v):
        return device(core * v + (1 - core) * y, z, core * x + (1 - core) * v, core)

    def on_three(v):
        return device(core * y + (1 - core) * v, z, core * v + (1 - core) * x, core)

    def turn(v, by, n):
        return lax.rem(v + by + n, n)

    plus, minus = on_three(turn(three, 1, ring)), on_three(turn(three, -1, ring))

    barrier = pltpu.get_barrier_semaphore()
    signal(barrier, partner)
    for d in range(1, deep):
        signal(barrier, on_z(turn(z, d, deep)))
    for d in range(1, ring):
        signal(barrier, on_two(turn(two, d, ring)))
    signal(barrier, plus)
    signal(barrier, minus)

    small = [
        pltpu.make_async_copy(idx_hbm, idx_ref, small_sem.at[0]),
        pltpu.make_async_copy(res_hbm, res_ref, small_sem.at[1]),
    ]
    for copy in small:
        copy.start()
    loads = []
    for c in range(chunks):
        here = slice(c * step, (c + 1) * step)
        loads.append(pltpu.make_async_copy(x_hbm.at[:, here], xs.at[:, here], load_sem.at[c]))
        loads[-1].start()

    small[0].wait()
    idx = idx_ref[...]
    offsets = own_offsets(idx, me, local_rows)
    column = stacked(offsets)
    frame = (
        lax.broadcasted_iota(jnp.int32, res_ref.shape, 0) * LANES + lane_of(res_ref.shape)
    ).astype(F32)
    small[1].wait()
    target = stacked([total(jnp.where(frame == v, res_ref[...], 0.0)) for v in offsets])
    rows = None
    for c in range(chunks):
        loads[c].wait()
        hot = jnp.where(
            lane_of((MOST, step)).astype(F32) + float(c * step) == column, 1.0, 0.0
        ).astype(BF16)
        part = lax.dot_general(
            hot, xs[:, c * step : (c + 1) * step], (((1,), (1,)), ((), ())),
            preferred_element_type=F32,
        )
        rows = part if rows is None else rows + part
    col = width - base
    tail = jnp.concatenate([rows[:, base:], jnp.zeros((MOST, LANES - col), F32)], axis=1)
    square = tail * tail
    for t in range(base // LANES):
        square = square + rows[:, t * LANES : (t + 1) * LANES] * rows[:, t * LANES : (t + 1) * LANES]
    norm = pieces(-0.5 * jnp.sum(square, axis=1, keepdims=True))
    wanted = pieces(target)
    lane = lane_of(tail.shape)
    for k in range(3):
        tail = jnp.where(lane == col + k, norm[k], tail)
        tail = jnp.where(lane == col + 3 + k, 1.0, tail)
        tail = jnp.where(lane == col + 6 + k, wanted[k], tail)
    pair[core, :, :base] = rows[:, :base]
    pair[core, :, base:] = tail

    pl.semaphore_wait(barrier, 1 + (deep - 1) + (ring - 1) + 2)

    first = send_to(pair.at[core], pair.at[core], pair_sem.at[0], pair_sem.at[1], partner)
    first.start()
    first.wait()
    mine = pl.ds(pl.multiple_of(core * half, half), half)
    both = jnp.concatenate([pair[0, :, mine], pair[1, :, mine]], axis=0)
    own[three, two, z] = both.astype(BF16)

    waits = []
    far = []
    for d in range(1, deep):
        there = own.at[three, two, z]
        far.append(send_to(there, there, far_send.at[d - 1], far_recv.at[d - 1], on_z(turn(z, d, deep))))
        far[-1].start()
    waits += far

    eye = eye_mask()
    owner = idx // local_rows
    row_owner = owner.astype(F32)
    home = lax.rem(owner, 2) * MOST + lax.rem(owner // (2 * GRID[2]), deep) * (2 * MOST)
    on_x = lax.rem(owner // 2, GRID[2])
    on_y = owner // (2 * GRID[2] * deep)
    spans = (2 * MOST * deep * ring, 2 * MOST * deep)
    slot_own = (home + (core * on_x + (1 - core) * on_y) * spans[0] + (core * on_y + (1 - core) * on_x) * spans[1]).astype(F32)
    slot_other = (home + (core * on_y + (1 - core) * on_x) * spans[0] + (core * on_x + (1 - core) * on_y) * spans[1]).astype(F32)
    lower = lane_of((LANES, LANES)) < lax.broadcasted_iota(jnp.int32, (LANES, LANES), 0)
    slots = place.shape[2]
    for t in range(size // LANES):
        here = slice(t * LANES, (t + 1) * LANES)
        holder = to_column(row_owner[t : t + 1, :], eye)
        count = jnp.where((holder == row_owner[t : t + 1, :]) & lower, 1.0, 0.0)
        for u in range(t):
            count = count + jnp.where(holder == row_owner[u : u + 1, :], 1.0, 0.0)
        rank = jnp.sum(count, axis=1, keepdims=True)
        for k, slot in enumerate((slot_own, slot_other)):
            at = (to_column(slot[t : t + 1, :], eye) + rank).astype(jnp.int32)
            place[k, here, :] = jnp.where(lane_of((LANES, slots)) == at, 1.0, 0.0).astype(BF16)

    def widen(c):
        here = slice(c * step, (c + 1) * step)
        value = xs[:, here].astype(F32)
        square = value * value
        parts = square[:8, :]
        for t in range(1, width // 8):
            parts = parts + square[t * 8 : (t + 1) * 8, :]
        norm = pieces(-0.5 * jnp.sum(parts, axis=0, keepdims=True))
        sub = lax.broadcasted_iota(jnp.int32, (8, step), 0)
        extra = jnp.where(sub < 3, 1.0, 0.0)
        for k in range(3):
            extra = jnp.where(sub == 3 + k, norm[k], extra)
        xa_ref[: width - 8, here] = xs[: width - 8, here]
        xa_ref[width - 8 :, here] = jnp.concatenate([value[width - 8 :, :], extra], axis=0).astype(BF16)

    other_cols = pl.ds(pl.multiple_of((1 - core) * half, half), half)

    def add_block(which, index, start):
        buf, cols = (own, mine) if which == 0 else (other, other_cols)
        k = pl.ds(pl.multiple_of(index * spans[0], spans[0]), spans[0])
        part = jnp.dot(
            place[which, :, k], buf[index].reshape(spans[0], half), preferred_element_type=F32
        )
        if start:
            block_ref[:, cols] = part
        else:
            block_ref[:, cols] = block_ref[:, cols] + part

    swaps = {}

    def swap(a, b):
        i, j = turn(three, a, ring), turn(two, b, ring)
        n = a * ring + b
        swaps[a, b] = send_to(own.at[i, j], other.at[i, j], swap_send.at[n], swap_recv.at[n], partner)
        swaps[a, b].start()

    straight = {}

    def onward(b):
        there = own.at[three, turn(two, b, ring)]
        for k, goal in enumerate((plus, minus)):
            copy = send_to(there, there, three_send.at[k, b], three_recv.at[k, b], goal)
            copy.start()
            straight[k, b] = copy

    relays = {}

    def relay(k, b):
        there = own.at[turn(three, -1 if k == 0 else 1, ring), turn(two, b, ring)]
        n = {0: 0, 1: 1, 3: 2, 2: 3}[b]
        copy = send_to(there, there, relay_send.at[n], relay_recv.at[n], plus if k == 0 else minus)
        copy.start()
        relays[b] = copy

    for copy in far:
        copy.wait_recv()
    second = {}
    for d in (1, 3, 2):
        there = own.at[three, two]
        second[d] = send_to(there, there, two_send.at[d - 1], two_recv.at[d - 1], on_two(turn(two, -d, ring)))
        second[d].start()
    onward(0)
    swap(0, 0)
    for c in range(chunks // 2):
        widen(c)
    for d in (1, 3):
        second[d].wait_recv()
        onward(d)
        swap(0, d)
    straight[0, 0].wait_recv()
    relay(0, 0)
    swap(3, 0)
    straight[1, 0].wait_recv()
    swap(1, 0)
    second[2].wait_recv()
    onward(2)
    swap(0, 2)
    add_block(0, three, True)
    straight[0, 1].wait_recv()
    relay(0, 1)
    swap(3, 1)
    straight[1, 3].wait_recv()
    relay(1, 3)
    swap(1, 3)
    straight[1, 1].wait_recv()
    swap(1, 1)
    straight[0, 3].wait_recv()
    swap(3, 3)
    for c in range(chunks // 2, chunks):
        widen(c)
    straight[1, 2].wait_recv()
    relay(1, 2)
    swap(1, 2)
    straight[0, 2].wait_recv()
    swap(3, 2)
    add_block(0, turn(three, 1, ring), False)
    add_block(0, turn(three, -1, ring), False)
    for b in range(ring):
        swaps[0, b].wait_recv()
    add_block(1, two, True)
    for b in (0, 1, 3, 2):
        relays[b].wait_recv()
        swap(2, b)
    add_block(0, turn(three, 2, ring), False)
    for a in (1, 3, 2):
        for b in range(ring):
            swaps[a, b].wait_recv()
        add_block(1, turn(two, a, ring), False)
    for copy in waits + list(second.values()) + list(straight.values()) + list(relays.values()) + list(swaps.values()):
        copy.wait_send()


def solve_kernel(width, scale, shift, block_ref, b_ref, coef_ref, columns_ref, swapped, system):
    size = b_ref.shape[0]
    groups = size // LANES
    base = WIDE - LANES
    col = width - base
    eye = eye_mask()
    tail = block_ref[:, base:]
    lane = lane_of(tail.shape)
    target_cols = jnp.sum(
        jnp.where((lane >= col + 6) & (lane < col + 9), tail, 0.0), axis=1, keepdims=True
    )
    tail = jnp.where(lane < col + 6, tail, 0.0)
    moved = pltpu.roll(tail, 3, 1)
    swap = jnp.where(lane < col, tail, jnp.where(lane < col + 3, 1.0, jnp.where(lane < col + 6, moved, 0.0)))
    plain = block_ref[:, :base].astype(BF16)
    b_ref[:, :base] = plain
    b_ref[:, base:] = tail.astype(BF16)
    swapped[:, :base] = plain
    swapped[:, base:] = swap.astype(BF16)
    inner = lax.dot_general(
        b_ref[...], swapped[...], (((1,), (1,)), ((), ())), preferred_element_type=F32
    )
    system[...] = jnp.exp2(inner * (2.0 * scale * LOG2E))
    for t in range(groups):
        here = slice(t * LANES, (t + 1) * LANES)
        system[here, here] = system[here, here] + jnp.where(eye, shift, 0.0)

    target = jnp.concatenate(
        [to_row(target_cols[t * LANES : (t + 1) * LANES], eye) for t in range(groups)], axis=0
    )
    top = jnp.max(jnp.max(jnp.abs(target), axis=1, keepdims=True), axis=0, keepdims=True)
    top = jnp.where(top > 0.0, top, 1.0)
    target = target / top

    def apply(p):
        rows = []
        for t in range(groups):
            acc = system[t * LANES : (t + 1) * LANES, :LANES] * p[:1, :]
            for u in range(1, groups):
                acc = acc + system[t * LANES : (t + 1) * LANES, u * LANES : (u + 1) * LANES] * p[u : u + 1, :]
            rows.append(to_row(jnp.sum(acc, axis=1, keepdims=True), eye))
        return jnp.concatenate(rows, axis=0)

    first = total(target * target)
    bound = first * 1e-12

    def going(carry):
        step, _, _, _, norm = carry
        return (step < 4 * size) & (jnp.sum(norm - bound) > 0.0)

    def advance(carry):
        step, x, r, p, norm = carry
        q = apply(p)
        alpha = norm / total(p * q)
        x = x + alpha * p
        r = r - alpha * q
        fresh = total(r * r)
        p = r + (fresh / norm) * p
        return step + 1, x, r, p, fresh

    out = lax.while_loop(
        going, advance, (jnp.int32(0), jnp.zeros_like(target), target, target, first)
    )
    coef = out[1] * top
    coef_ref[...] = coef
    for t in range(groups):
        columns_ref[t * LANES : (t + 1) * LANES, :] = jnp.broadcast_to(
            to_column(coef[t : t + 1, :], eye), (LANES, LANES)
        )


def panel_kernel(
    tile, scale, frames, columns, b_ref, x_ref, res_hbm, out_ref, rms_ref,
    res_ref, res_sem, line_a, line_b, send_a, recv_a, send_b, recv_b,
):
    rows = x_ref.shape[1]
    me, y, z, x, core = position()
    spot_a = z * 2 + core
    spot_b = y * GRID[2] + x
    count_a = line_a.shape[0]
    count_b = line_b.shape[0]

    def peer_a(d):
        v = lax.rem(spot_a + d, count_a)
        return device(y, v // 2, x, lax.rem(v, 2))

    def peer_b(d):
        v = lax.rem(spot_b + d, count_b)
        return device(v // GRID[2], z, lax.rem(v, GRID[2]), core)

    barrier = pltpu.get_barrier_semaphore()

    def greet_a(d, _):
        signal(barrier, peer_a(d))
        return 0

    def greet_b(d, _):
        signal(barrier, peer_b(d))
        return 0

    lax.fori_loop(1, count_a, greet_a, 0)
    lax.fori_loop(1, count_b, greet_b, 0)

    load = pltpu.make_async_copy(res_hbm, res_ref, res_sem)
    load.start()
    load.wait()

    def step(i, _):
        here = pl.ds(pl.multiple_of(i * tile, tile), tile)
        inner = jnp.dot(b_ref[:, :DEEP], x_ref[:, here], preferred_element_type=F32)
        value = jnp.exp2(inner * (2.0 * scale * LOG2E))
        for k in range(tile // LANES):
            change = jnp.sum(value[:, k * LANES : (k + 1) * LANES] * columns[...], axis=0, keepdims=True)
            at = pl.ds(i * (tile // LANES) + k, 1)
            out_ref[at, :] = res_ref[at, :] - change
        return 0

    lax.fori_loop(0, rows // tile, step, 0)
    updated = out_ref[...]
    square = updated * updated
    parts = square[:8, :]
    for t in range(1, square.shape[0] // 8):
        parts = parts + square[t * 8 : (t + 1) * 8, :]
    line_a[spot_a] = jnp.broadcast_to(total(parts), (1, LANES))

    pl.semaphore_wait(barrier, count_a + count_b - 2)

    def exchange(line, spot, send, recv, peer):
        def copy(d):
            return send_to(line.at[spot], line.at[spot], send.at[d - 1], recv.at[d - 1], peer(d))

        def begin(d, _):
            copy(d).start()
            return 0

        def end(d, _):
            copy(d).wait()
            return 0

        lax.fori_loop(1, line.shape[0], begin, 0)
        lax.fori_loop(1, line.shape[0], end, 0)
        out = line[0]
        for k in range(1, line.shape[0]):
            out = out + line[k]
        return out

    line_b[spot_b] = exchange(line_a, spot_a, send_a, recv_a, peer_a)
    whole = exchange(line_b, spot_b, send_b, recv_b, peer_b)
    rms_ref[...] = jnp.sqrt(whole / frames + 1e-06)


VM = pl.BlockSpec(memory_space=pltpu.VMEM)
HBM = pl.BlockSpec(memory_space=pltpu.HBM)
DMA = pltpu.SemaphoreType.DMA


def in_hbm(value):
    return pltpu.with_memory_space_constraint(value, pltpu.HBM)


def gather(idx, features, residual):
    width, local_rows = features.shape
    size = idx.shape[0]
    slots = 2 * GRID[0] * GRID[1] * GRID[2] * MOST
    part = (GRID[0], GRID[2], GRID[1], 2 * MOST, WIDE // 2)
    return pl.pallas_call(
        functools.partial(gather_kernel, local_rows),
        out_shape=(
            jax.ShapeDtypeStruct((DEEP, local_rows), BF16),
            jax.ShapeDtypeStruct((size, WIDE), F32),
        ),
        in_specs=[HBM, HBM, HBM],
        out_specs=(VM, VM),
        scratch_shapes=[
            pltpu.VMEM((size // LANES, LANES), jnp.int32),
            pltpu.VMEM((local_rows // LANES, LANES), F32),
            DMA((2,)),
            pltpu.VMEM((width, local_rows), BF16),
            pltpu.VMEM((2, size, slots), BF16),
            pltpu.VMEM((2, MOST, WIDE), F32),
            pltpu.VMEM(part, BF16),
            pltpu.VMEM(part, BF16),
            DMA((4,)),
            DMA((2,)),
            DMA((GRID[1] - 1,)),
            DMA((GRID[1] - 1,)),
            DMA((3,)),
            DMA((3,)),
            DMA((2, 4)),
            DMA((2, 4)),
            DMA((4,)),
            DMA((4,)),
            DMA((16,)),
            DMA((16,)),
        ],
        compiler_params=pltpu.CompilerParams(
            vmem_limit_bytes=36 << 20, collective_id=0, has_side_effects=True
        ),
        name="gather",
    )(
        in_hbm(idx.reshape(size // LANES, LANES)),
        in_hbm(features),
        in_hbm(residual.reshape(local_rows // LANES, LANES)),
    )


def solve(block, width, scale):
    size = block.shape[0]
    return pl.pallas_call(
        functools.partial(solve_kernel, width, scale, 0.1),
        out_shape=(
            jax.ShapeDtypeStruct((size, WIDE), BF16),
            jax.ShapeDtypeStruct((size // LANES, LANES), F32),
            jax.ShapeDtypeStruct((size, LANES), F32),
        ),
        in_specs=[VM],
        out_specs=(VM, VM, VM),
        scratch_shapes=[
            pltpu.VMEM((size, WIDE), BF16),
            pltpu.VMEM((size, size), F32),
        ],
        compiler_params=pltpu.CompilerParams(vmem_limit_bytes=36 << 20),
        name="solve",
    )(block)


def panel(columns, block, wide, residual, scale):
    rows = wide.shape[1]
    tile = 1024
    return pl.pallas_call(
        functools.partial(panel_kernel, tile, scale, float(rows * lax.axis_size("rows"))),
        out_shape=(
            jax.ShapeDtypeStruct((rows // LANES, LANES), F32),
            jax.ShapeDtypeStruct((1, LANES), F32),
        ),
        in_specs=[VM, VM, VM, HBM],
        out_specs=(VM, VM),
        scratch_shapes=[
            pltpu.VMEM((rows // LANES, LANES), F32),
            DMA,
            pltpu.VMEM((2 * GRID[1], 1, LANES), F32),
            pltpu.VMEM((GRID[0] * GRID[2], 1, LANES), F32),
            DMA((15,)),
            DMA((15,)),
            DMA((15,)),
            DMA((15,)),
        ],
        compiler_params=pltpu.CompilerParams(
            vmem_limit_bytes=36 << 20, collective_id=1, has_side_effects=True
        ),
        name="panel",
    )(columns, block, wide, in_hbm(residual.reshape(rows // LANES, LANES)))


def on_device(features, residual, block_index):
    local_rows, width = features.shape
    scale = 2.0 / width
    wide, block = gather(block_index, features.T, residual)
    block, coef, columns = solve(block, width, scale)
    updated, rms = panel(columns, block, wide, residual, scale)
    return (updated.reshape(local_rows), coef.reshape(-1), rms[0, 0])


def solution(mesh):
    in_specs = (P("rows", None), P("rows"), P())
    out_specs = (P("rows"), P(), P())
    return jax.shard_map(
        on_device, mesh=mesh, in_specs=in_specs, out_specs=out_specs, check_vma=False
    )
```
